1024 devices in a mesh: seq: 64 (over x_hi, z, core), chan: 16 (over y, x_lo).
Axes of the slice: x: 8 (x_hi: 4, x_lo: 2; x = x_hi * 2 + x_lo), y: 8, z: 8, core: 2. Of those that a mesh axis runs over, the one named last changes fastest.
Arguments:
- tokens: bfloat16 [20480, 4096], P('seq', 'chan'), may hold values from -70 to 70
- in_weight: bfloat16 [4096, 3, 4096], P(None, None, 'chan'), may hold values from -0.09375 to 0.09375
- short_filter: float32 [3, 3, 4096], P(None, None, 'chan'), may hold values from -2 to 2
- long_filter: bfloat16 [256, 128], P('chan'), may hold values from -0.5 to 0.5
- skip_gain: float32 [4096], P('chan'), may hold values from -4 to 4
- out_weight: bfloat16 [4096, 4096], P('chan'), may hold values from -0.125 to 0.125
Outputs:
- mixed: bfloat16 [20480, 4096], P('seq', 'chan')
The draws below stay inside these ranges and needn't reach their ends.
All inputs are finite; a program needn't handle non-finite values.
Results may differ from the reference program's by a relative error of at most 0.018.
Values may be sent and summed in bfloat16 or wider, within the bound.
No kernel may reach another device: no remote copies, remote signals or barrier semaphores. Data moves between devices by JAX's collectives and lax.ppermute only.
A program may use at most 64 MiB of HBM per device.

```python
import math
import jax
import jax.numpy as jnp
from jax import lax

D = 4096
CH = 4096
GROUP = 16
FILT = 128
SHORT = 3
TOKENS = 20480
GROUPS = 256


def draw_tokens(key, part):
    key_list = jax.random.split(key, 3)
    base_values = jnp.clip(jax.random.normal(key_list[0], (TOKENS, D), jnp.float32), -4.0, 4.0)
    row_scale = jnp.exp(jax.random.uniform(key_list[1], (TOKENS, 1), jnp.float32, 0.0, math.log(10.0)))
    column_scale = jnp.exp(jax.random.uniform(key_list[2], (1, D), jnp.float32, 0.0, math.log(10.0)))
    return (base_values * row_scale * column_scale * 0.1).astype(jnp.bfloat16)


def strengthened(drawn, stream_key, source, target, shards_of, factor):
    def block_of(position):
        return (jnp.arange(drawn.shape[position]) // (drawn.shape[position] // shards_of)).reshape((-1,) + (1,) * (drawn.ndim - 1 - position))

    first = jax.random.permutation(stream_key, shards_of)[block_of(target)]
    other_side = (block_of(target) + shards_of // 2) % shards_of
    return jnp.where((block_of(source) == first) | (block_of(source) == other_side), factor * drawn, drawn)


def level_of(key, shape, cuts, smallest, largest):
    def one(dim, blocks):
        steps = jax.random.uniform(jax.random.fold_in(jax.random.fold_in(key, 6), dim), (blocks,), jnp.float32, smallest / len(cuts), largest / len(cuts))
        return jnp.repeat(jnp.exp(steps), shape[dim] // blocks).reshape((-1,) + (1,) * (len(shape) - dim - 1))

    factor_of = one(*cuts[0])
    for cut in cuts[1:]:
        factor_of = factor_of * one(*cut)
    return factor_of


def bell_draw(key, extent, deviation, limit, shards=(), held_as=jnp.bfloat16):
    values = jax.random.normal(key, extent, jnp.float32) * deviation
    if len(shards) > 0:
        values = level_of(key, extent, shards, -0.22, 0.18) * values
    return jnp.clip(values, min=-limit, max=limit).astype(held_as)


def bell_draw_with(rng, shape, width, most, shards, heavy, held_as=jnp.bfloat16):
    result = width * jax.random.normal(rng, shape, jnp.float32)
    if shards:
        result = result * level_of(rng, shape, shards, -0.22, 0.18)
    return jnp.clip(strengthened(result, jax.random.fold_in(rng, 3), *heavy), -most, most).astype(held_as)


def setup_inputs(seed: int = 0) -> dict:
    keys = jax.random.split(jax.random.key(seed), 7)
    tokens = draw_tokens(jax.random.fold_in(keys[6], 71), 0)
    in_weight = bell_draw(keys[1], (D, 3, CH), D ** -0.5, 0.09375, ((2, 16),))
    short_filter = bell_draw(keys[2], (SHORT, 3, CH), 0.4, 2.0, ((2, 16),), jnp.float32)
    long_filter = bell_draw(keys[3], (GROUPS, FILT), 0.09, 0.5, ((0, 16),))
    skip_gain = bell_draw(keys[4], (CH,), 1.0, 4.0, ((0, 16),), jnp.float32)
    out_weight = bell_draw_with(keys[5], (CH, D), CH ** -0.5, 0.125, ((0, 16),), (0, 1, 16, 2.0))
    return dict(tokens=tokens, in_weight=in_weight, short_filter=short_filter, long_filter=long_filter, skip_gain=skip_gain, out_weight=out_weight)


def short_stream(projected, short_filter, stream):
    widened = projected[:, stream, :].astype(jnp.float32)
    padded = jnp.pad(widened, ((SHORT - 1, 0), (0, 0)))
    summed = jnp.zeros((TOKENS, CH), jnp.float32)
    for step_back in range(SHORT):
        summed = summed + short_filter[step_back, stream] * padded[SHORT - 1 - step_back:SHORT - 1 - step_back + TOKENS]
    return summed

def reference(tokens, in_weight, short_filter, long_filter, skip_gain, out_weight):
    panel_sum = jnp.dot(tokens, in_weight.reshape(D, 3 * CH), preferred_element_type=jnp.float32)
    widened = tokens.astype(jnp.float32)
    inverse_rms = lax.rsqrt(lax.optimization_barrier(jnp.mean(widened * widened, axis=1, keepdims=True)) + 1e-06)
    projected = (panel_sum * inverse_rms).astype(jnp.bfloat16).reshape(TOKENS, 3, CH)
    queries = short_stream(projected, short_filter, 0)
    keys_part = short_stream(projected, short_filter, 1)
    values_part = short_stream(projected, short_filter, 2)
    gated = (keys_part * values_part).astype(jnp.bfloat16)
    gated_wide = gated.astype(jnp.float32)
    channel_taps = jnp.repeat(long_filter.astype(jnp.float32), GROUP, axis=0)
    padded = jnp.pad(gated_wide, ((FILT - 1, 0), (0, 0)))

    def add_tap(step_back, summed):
        shifted = lax.dynamic_slice_in_dim(padded, FILT - 1 - step_back, TOKENS, 0)
        return summed + channel_taps[:, step_back] * shifted
    long_mixed = lax.fori_loop(0, FILT, add_tap, jnp.zeros((TOKENS, CH), jnp.float32))
    long_mixed = long_mixed + skip_gain * gated_wide
    hidden = (queries * long_mixed).astype(jnp.bfloat16)
    return jnp.dot(hidden, out_weight, preferred_element_type=jnp.float32).astype(jnp.bfloat16)
```

```python
import jax
import jax.numpy as jnp
from jax import lax
from jax.experimental import pallas as pl
from jax.experimental.pallas import tpu as pltpu
from jax.sharding import PartitionSpec as P


YS = 8
XS = 2
LATE = 128
BLOCK = 64
HALO = 136
VMEM = pltpu.VMEM

Y_GROUPS = [[y * XS + x for y in range(YS)] for x in range(XS)]
X_PAIRS = [(y * XS + x, y * XS + 1 - x) for y in range(YS) for x in range(XS)]


def swap_x(value):
    return lax.ppermute(value, "chan", X_PAIRS)


def exchange_y(value):
    return lax.all_to_all(value, "chan", 0, 0, tiled=True, axis_index_groups=Y_GROUPS)


def shifted(value, axis):
    count = lax.axis_size(axis)
    return lax.ppermute(value, axis, [(source, source + 1) for source in range(count - 1)])


def project_kernel(x_ref, own1, oth1, pair2, weight, out, acc, squares):
    step = pl.program_id(0)
    x = x_ref[0]
    first = pl.multiple_of(x * 256, 256)
    second = pl.multiple_of((1 - x) * 256, 256)
    own = jnp.concatenate([own1[0], pair2[0, 0]], axis=0)
    oth = jnp.concatenate([oth1[0], pair2[0, 1]], axis=0)
    both = jnp.concatenate([own, oth], axis=1)
    wide = both.astype(jnp.float32)
    wide = wide * wide
    part = wide[:, :128]
    for k in range(1, 4):
        part = part + wide[:, 128 * k : 128 * k + 128]

    @pl.when(step == 0)
    def _():
        squares[...] = part

    @pl.when(step > 0)
    def _():
        squares[...] += part

    for i in range(3):
        w = jnp.concatenate([weight[i, pl.ds(first, 256), :], weight[i, pl.ds(second, 256), :]], 0)
        product = jnp.dot(both, w, preferred_element_type=jnp.float32)

        @pl.when(step == 0)
        def _():
            acc[i] = product

        @pl.when(step > 0)
        def _():
            acc[i] += product

    @pl.when(step == YS - 1)
    def _():
        mean = jnp.sum(squares[...], axis=1, keepdims=True) / (YS * XS * 256)
        scale = lax.rsqrt(mean + 1e-06)
        for i in range(3):
            out[:, 256 * i : 256 * i + 256] = (acc[i] * scale).astype(jnp.bfloat16)


def project(x, own1, oth1, pair2, weight):
    rows = own1.shape[1] + pair2.shape[2]
    return pl.pallas_call(
        project_kernel,
        grid=(YS,),
        in_specs=[
            pl.BlockSpec(memory_space=pltpu.SMEM),
            pl.BlockSpec((1,) + own1.shape[1:], lambda k: (k, 0, 0)),
            pl.BlockSpec((1,) + oth1.shape[1:], lambda k: (k, 0, 0)),
            pl.BlockSpec((1,) + pair2.shape[1:], lambda k: (k, 0, 0, 0)),
            pl.BlockSpec((3, 512, 256), lambda k: (0, k, 0)),
        ],
        out_specs=pl.BlockSpec((rows, 768), lambda k: (0, 0)),
        out_shape=jax.ShapeDtypeStruct((rows, 768), jnp.bfloat16),
        scratch_shapes=[VMEM((3, rows, 256), jnp.float32), VMEM((rows, 128), jnp.float32)],
        name="project",
    )(x, own1, oth1, pair2, weight)


def mix_kernel(x_ref, proj, halo, short, taps, skip, weight, send, keep, pair, wide, gated, table, mixed):
    rows = proj.shape[0]
    x = x_ref[0]
    wide[0:HALO] = halo[...].astype(jnp.float32)
    wide[HALO:] = proj[...].astype(jnp.float32)

    def stream(i, start, count):
        lanes = slice(256 * i, 256 * i + 256)
        total = short[0, i : i + 1, :] * wide[start : start + count, lanes]
        for back in range(1, 3):
            total += short[back, i : i + 1, :] * wide[start - back : start - back + count, lanes]
        return total

    gated_rows = rows + 128
    product = stream(1, HALO - 128, gated_rows) * stream(2, HALO - 128, gated_rows)
    gated[0:gated_rows] = product.astype(jnp.bfloat16)
    gated[gated_rows:] = jnp.zeros((gated.shape[0] - gated_rows, 256), jnp.bfloat16)
    for g in range(16):
        line = jnp.broadcast_to(taps[g : g + 1, :], (BLOCK, 256))
        rolled = pltpu.roll(line, 1, 1, stride=1, stride_axis=0)
        table[BLOCK * g : BLOCK * g + BLOCK] = rolled.astype(jnp.bfloat16)
    group = lax.broadcasted_iota(jnp.int32, (BLOCK, 256), 1) // 16
    for b in range(rows // BLOCK):
        window = gated[BLOCK * b : BLOCK * b + 256]
        every = jnp.dot(table[...], window, preferred_element_type=jnp.float32)
        total = every[0:BLOCK]
        for g in range(1, 16):
            total = jnp.where(group == g, every[BLOCK * g : BLOCK * g + BLOCK], total)
        own = gated[BLOCK * b + 128 : BLOCK * b + 128 + BLOCK].astype(jnp.float32)
        total = total + skip[...] * own
        queries = stream(0, HALO + BLOCK * b, BLOCK)
        mixed[BLOCK * b : BLOCK * b + BLOCK] = (queries * total).astype(jnp.bfloat16)
    early = rows - LATE
    low = mixed[0:early]
    high = mixed[early:]
    for y in range(YS):
        mine = pl.multiple_of(y * 512 + x * 256, 256)
        other = pl.multiple_of(y * 512 + 256 - x * 256, 256)
        send[y] = jnp.dot(low, weight[:, pl.ds(other, 256)], preferred_element_type=jnp.float32).astype(jnp.bfloat16)
        keep[y] = jnp.dot(low, weight[:, pl.ds(mine, 256)], preferred_element_type=jnp.float32).astype(jnp.bfloat16)
        pair[y, 0] = jnp.dot(high, weight[:, pl.ds(mine, 256)], preferred_element_type=jnp.float32).astype(jnp.bfloat16)
        pair[y, 1] = jnp.dot(high, weight[:, pl.ds(other, 256)], preferred_element_type=jnp.float32).astype(jnp.bfloat16)


def mix(x, proj, halo, short, taps, skip, weight):
    rows = proj.shape[0]
    early = rows - LATE
    whole = pl.BlockSpec(memory_space=VMEM)
    return pl.pallas_call(
        mix_kernel,
        in_specs=[pl.BlockSpec(memory_space=pltpu.SMEM)] + [whole] * 6,
        out_specs=[whole] * 3,
        out_shape=[
            jax.ShapeDtypeStruct((YS, early, 256), jnp.bfloat16),
            jax.ShapeDtypeStruct((YS, early, 256), jnp.bfloat16),
            jax.ShapeDtypeStruct((YS, 2, LATE, 256), jnp.bfloat16),
        ],
        scratch_shapes=[
            VMEM((HALO + rows, 768), jnp.float32),
            VMEM((rows + 256, 256), jnp.bfloat16),
            VMEM((16 * BLOCK, 256), jnp.bfloat16),
            VMEM((rows, 256), jnp.bfloat16),
        ],
        name="mix",
    )(x, proj, halo, short, taps, skip, weight)


def body(tokens, in_weight, short_filter, long_filter, skip_gain, out_weight):
    rows = tokens.shape[0]
    early = rows - LATE
    x = (lax.axis_index("chan") % XS).astype(jnp.int32)
    x_ref = x[None]
    weight = jnp.transpose(in_weight, (1, 0, 2))
    taps = jnp.pad(jnp.flip(long_filter, 1).astype(jnp.float32), ((0, 0), (0, 128)))
    skip = skip_gain[None]

    top, tail = tokens[:early], tokens[early:]
    tail_other = swap_x(tail)
    own1 = exchange_y(jnp.broadcast_to(top[None], (YS,) + top.shape))
    tail_other, own1 = lax.optimization_barrier((tail_other, own1))
    oth1 = swap_x(own1)
    both = jnp.stack([tail, tail_other])
    pair2 = exchange_y(jnp.broadcast_to(both[None], (YS,) + both.shape))

    proj = project(x_ref, own1, oth1, pair2, weight)
    halo = shifted(proj[rows - HALO :], "seq")
    send, keep, pair = mix(x_ref, proj, halo, short_filter, taps, skip, out_weight)

    received = swap_x(send)
    pair = exchange_y(pair)
    sums = jnp.sum(pair.astype(jnp.float32), axis=0)
    late_send = sums[1].astype(jnp.bfloat16)
    late_send, received = lax.optimization_barrier((late_send, received))
    late_received = swap_x(late_send)
    merged = (keep.astype(jnp.float32) + received.astype(jnp.float32)).astype(jnp.bfloat16)
    merged = exchange_y(merged)
    early_out = jnp.sum(merged.astype(jnp.float32), axis=0).astype(jnp.bfloat16)
    late_out = (sums[0] + late_received.astype(jnp.float32)).astype(jnp.bfloat16)
    return jnp.concatenate([early_out, late_out], axis=0)


def solution(mesh):
    in_specs = (
        P("seq", "chan"),
        P(None, None, "chan"),
        P(None, None, "chan"),
        P("chan", None),
        P("chan"),
        P("chan", None),
    )
    out_specs = P("seq", "chan")
    return jax.shard_map(body, mesh=mesh, in_specs=in_specs, out_specs=out_specs, check_vma=False)
```

```python
import jax
import jax.numpy as jnp
from jax import lax
from jax.experimental import pallas as pl
from jax.experimental.pallas import tpu as pltpu
from jax.sharding import PartitionSpec as P


YS = 8
XS = 2
LATE_IN = 128
LATE_OUT = 160
BLOCK = 32
HALO = 136
VMEM = pltpu.VMEM
F32 = jnp.float32
BF16 = jnp.bfloat16

Y_GROUPS = [[y * XS + x for y in range(YS)] for x in range(XS)]
X_PAIRS = [(y * XS + x, y * XS + 1 - x) for y in range(YS) for x in range(XS)]


def swap_x(value):
    return lax.ppermute(value, "chan", X_PAIRS)


def exchange_y(value):
    return lax.all_to_all(value, "chan", 0, 0, tiled=True, axis_index_groups=Y_GROUPS)


def shifted(value, axis):
    count = lax.axis_size(axis)
    return lax.ppermute(value, axis, [(source, source + 1) for source in range(count - 1)])


def in_vmem(value):
    return pltpu.with_memory_space_constraint(value, VMEM)


def project_rows(x, own, oth, weight, ready, store):
    rows = own(0).shape[0]
    squares = jnp.zeros((rows, 128), F32)
    for y in range(YS):
        for piece in (own(y), oth(y)):
            wide = piece.astype(F32)
            wide = wide * wide
            squares = squares + wide[:, :128] + wide[:, 128:]
    mean = jnp.sum(squares, axis=1, keepdims=True) / (YS * XS * 256)
    scale = lax.rsqrt(mean + 1e-06)
    for i in range(3):
        ready(i)
        total = jnp.zeros((rows, 256), F32)
        for y in range(YS):
            first = pl.multiple_of(y * 512 + x * 256, 256)
            second = pl.multiple_of(y * 512 + 256 - x * 256, 256)
            total = total + jnp.dot(own(y), weight[i, pl.ds(first, 256), :], preferred_element_type=F32)
            total = total + jnp.dot(oth(y), weight[i, pl.ds(second, 256), :], preferred_element_type=F32)
        store(i, (total * scale).astype(BF16))


def early_kernel(
    x_ref, own_hbm, oth_hbm, weight_hbm, taps, out_hbm, table_hbm,
    own1, oth1, weight, out, table, arrived, sent
):
    own_fetch = pltpu.make_async_copy(own_hbm, own1, arrived.at[3])
    oth_fetch = pltpu.make_async_copy(oth_hbm, oth1, arrived.at[4])
    fetches = [pltpu.make_async_copy(weight_hbm.at[i], weight.at[i], arrived.at[i]) for i in range(3)]
    for fetch in [own_fetch, oth_fetch] + fetches:
        fetch.start()
    for g in range(16):
        line = jnp.broadcast_to(taps[g : g + 1, :], (BLOCK, 256))
        rolled = pltpu.roll(line, 1, 1, stride=1, stride_axis=0)
        table[BLOCK * g : BLOCK * g + BLOCK] = rolled.astype(BF16)
    table_send = pltpu.make_async_copy(table, table_hbm, sent.at[0])
    table_send.start()
    own_fetch.wait()
    oth_fetch.wait()

    def ready(i):
        fetches[i].wait()

    def store(i, value):
        out[:, 256 * i : 256 * i + 256] = value

    project_rows(x_ref[0], lambda y: own1[y], lambda y: oth1[y], weight, ready, store)
    out_send = pltpu.make_async_copy(out, out_hbm, sent.at[1])
    out_send.start()
    out_send.wait()
    table_send.wait()


def mix_rows(wide, base, gated, table, short, skip, mixed, count):
    def stream(i, start, length):
        lanes = slice(256 * i, 256 * i + 256)
        total = short[0, i : i + 1, :] * wide[start : start + length, lanes]
        for back in range(1, 3):
            total += short[back, i : i + 1, :] * wide[start - back : start - back + length, lanes]
        return total

    product = stream(1, base, count + 128) * stream(2, base, count + 128)
    gated[0 : count + 128] = product.astype(BF16)
    gated[count + 128 :] = jnp.zeros((gated.shape[0] - count - 128, 256), BF16)
    group = lax.broadcasted_iota(jnp.int32, (BLOCK, 256), 1) // 16
    for b in range(count // BLOCK):
        window = gated[BLOCK * b : BLOCK * b + 256]
        every = jnp.dot(table[...], window, preferred_element_type=F32)
        total = every[0:BLOCK]
        for g in range(1, 16):
            total = jnp.where(group == g, every[BLOCK * g : BLOCK * g + BLOCK], total)
        own = gated[BLOCK * b + 128 : BLOCK * b + 128 + BLOCK].astype(F32)
        total = total + skip[...] * own
        queries = stream(0, base + 128 + BLOCK * b, BLOCK)
        mixed[BLOCK * b : BLOCK * b + BLOCK] = (queries * total).astype(BF16)


def out_rows(x, value, weight, store):
    for y in range(YS):
        mine = pl.multiple_of(y * 512 + x * 256, 256)
        other = pl.multiple_of(y * 512 + 256 - x * 256, 256)
        store(y, 0, jnp.dot(value, weight[:, pl.ds(mine, 256)], preferred_element_type=F32).astype(BF16))
        store(y, 1, jnp.dot(value, weight[:, pl.ds(other, 256)], preferred_element_type=F32).astype(BF16))


def late_kernel(
    x_ref, pair2, weight_hbm, proj_hbm, table_hbm, short, skip, out_hbm, tail_hbm, pair_hbm,
    weight, proj1, table, out_weight, wide, gated, mixed, tail, pair, arrived, sent
):
    fetches = [pltpu.make_async_copy(weight_hbm.at[i], weight.at[i], arrived.at[i]) for i in range(3)]
    proj_fetch = pltpu.make_async_copy(proj_hbm, proj1, arrived.at[3])
    table_fetch = pltpu.make_async_copy(table_hbm, table, arrived.at[4])
    out_fetch = pltpu.make_async_copy(out_hbm, out_weight, arrived.at[5])
    for fetch in fetches + [proj_fetch, table_fetch, out_fetch]:
        fetch.start()
    early = proj1.shape[0]
    late = pair2.shape[2]
    rows = early + late

    def ready(i):
        fetches[i].wait()

    def store(i, value):
        tail[HALO - late :, 256 * i : 256 * i + 256] = value
        wide[early:, 256 * i : 256 * i + 256] = value.astype(F32)

    project_rows(x_ref[0], lambda y: pair2[y, 0], lambda y: pair2[y, 1], weight, ready, store)
    proj_fetch.wait()
    wide[0:early] = proj1[...].astype(F32)
    tail[0 : HALO - late] = proj1[early + late - HALO :]
    tail_send = pltpu.make_async_copy(tail, tail_hbm, sent.at[YS])
    tail_send.start()
    table_fetch.wait()
    mix_rows(wide, rows - LATE_OUT - 128, gated, table, short, skip, mixed, LATE_OUT)
    out_fetch.wait()
    sends = [pltpu.make_async_copy(pair.at[y], pair_hbm.at[y], sent.at[y]) for y in range(YS)]

    def place(y, side, value):
        pair[y, side] = value
        if side == 1:
            sends[y].start()

    out_rows(x_ref[0], mixed[...], out_weight, place)
    for send in sends + [tail_send]:
        send.wait()


def edge_kernel(
    x_ref, halo, proj_hbm, table_hbm, short, skip, out_hbm, send_hbm, keep_hbm,
    proj1, table, out_weight, wide, gated, mixed, send, keep, arrived, sent
):
    count = mixed.shape[0]
    proj_fetch = pltpu.make_async_copy(proj_hbm.at[0:count], proj1, arrived.at[0])
    table_fetch = pltpu.make_async_copy(table_hbm, table, arrived.at[1])
    out_fetch = pltpu.make_async_copy(out_hbm, out_weight, arrived.at[2])
    for fetch in (proj_fetch, table_fetch, out_fetch):
        fetch.start()
    wide[0:HALO] = halo[...].astype(F32)
    proj_fetch.wait()
    wide[HALO:] = proj1[...].astype(F32)
    table_fetch.wait()
    mix_rows(wide, HALO - 128, gated, table, short, skip, mixed, count)
    out_fetch.wait()

    sends = [pltpu.make_async_copy(send.at[y], send_hbm.at[y], sent.at[y]) for y in range(YS)]
    keeps = [pltpu.make_async_copy(keep.at[y], keep_hbm.at[y], sent.at[YS + y]) for y in range(YS)]

    def place(y, side, value):
        if side == 0:
            keep[y] = value
            keeps[y].start()
        else:
            send[y] = value
            sends[y].start()

    out_rows(x_ref[0], mixed[...], out_weight, place)
    for copy in sends + keeps:
        copy.wait()


WHOLE = pl.BlockSpec(memory_space=VMEM)
ANY = pl.BlockSpec(memory_space=pltpu.HBM)
SCALAR = pl.BlockSpec(memory_space=pltpu.SMEM)
PARAMS = pltpu.CompilerParams(vmem_limit_bytes=55 << 20)


def struct(*shape):
    return jax.ShapeDtypeStruct(shape, BF16)


def body(tokens, in_weight, short_filter, long_filter, skip_gain, out_weight):
    rows = tokens.shape[0]
    early_in = rows - LATE_IN
    early_out = rows - LATE_OUT
    x = (lax.axis_index("chan") % XS).astype(jnp.int32)[None]
    weight = jnp.transpose(in_weight, (1, 0, 2))
    taps = jnp.pad(jnp.flip(long_filter, 1).astype(F32), ((0, 0), (0, 128)))
    skip = skip_gain[None]

    top, tail = tokens[:early_in], tokens[early_in:]
    tail_other = swap_x(tail)
    own1 = exchange_y(jnp.broadcast_to(top[None], (YS,) + top.shape))
    tail_other, own1 = lax.optimization_barrier((tail_other, own1))
    oth1 = swap_x(own1)
    both = jnp.stack([tail, tail_other])
    pair2 = exchange_y(jnp.broadcast_to(both[None], (YS,) + both.shape))

    weight_space = VMEM(weight.shape, BF16)
    table_space = VMEM((16 * BLOCK, 256), BF16)
    out_space = VMEM(out_weight.shape, BF16)
    copies = pltpu.SemaphoreType.DMA
    proj1, table = pl.pallas_call(
        early_kernel,
        in_specs=[SCALAR, ANY, ANY, ANY, WHOLE],
        out_specs=[ANY] * 2,
        out_shape=[struct(early_in, 768), struct(16 * BLOCK, 256)],
        scratch_shapes=[
            VMEM(own1.shape, BF16),
            VMEM(own1.shape, BF16),
            weight_space,
            VMEM((early_in, 768), BF16),
            table_space,
            copies((5,)),
            copies((2,)),
        ],
        compiler_params=PARAMS,
        name="early",
    )(x, own1, oth1, weight, taps)
    tail_rows, pair = pl.pallas_call(
        late_kernel,
        in_specs=[SCALAR, WHOLE, ANY, ANY, ANY, WHOLE, WHOLE, ANY],
        out_specs=[ANY, ANY],
        out_shape=[struct(HALO, 768), struct(YS, 2, LATE_OUT, 256)],
        scratch_shapes=[
            weight_space,
            VMEM((early_in, 768), BF16),
            table_space,
            out_space,
            VMEM((rows, 768), F32),
            VMEM((LATE_OUT + 256, 256), BF16),
            VMEM((LATE_OUT, 256), BF16),
            VMEM((HALO, 768), BF16),
            VMEM((YS, 2, LATE_OUT, 256), BF16),
            copies((6,)),
            copies((YS + 1,)),
        ],
        compiler_params=PARAMS,
        name="late",
    )(x, in_vmem(pair2), weight, proj1, table, short_filter, skip, out_weight)

    halo = shifted(tail_rows, "seq")
    pair = exchange_y(pair)
    send, keep = pl.pallas_call(
        edge_kernel,
        in_specs=[SCALAR, WHOLE, ANY, ANY, WHOLE, WHOLE, ANY],
        out_specs=[ANY] * 2,
        out_shape=[struct(YS, early_out, 256), struct(YS, early_out, 256)],
        scratch_shapes=[
            VMEM((early_out, 768), BF16),
            table_space,
            out_space,
            VMEM((HALO + early_out, 768), F32),
            VMEM((early_out + 256, 256), BF16),
            VMEM((early_out, 256), BF16),
            VMEM((YS, early_out, 256), BF16),
            VMEM((YS, early_out, 256), BF16),
            copies((3,)),
            copies((2 * YS,)),
        ],
        compiler_params=PARAMS,
        name="edge",
    )(x, in_vmem(halo), proj1, table, short_filter, skip, out_weight)

    received = swap_x(send)
    sums = jnp.sum(pair.astype(F32), axis=0)
    late_send = sums[1].astype(BF16)
    late_send, received = lax.optimization_barrier((late_send, received))
    late_received = swap_x(late_send)
    merged = exchange_y((keep.astype(F32) + received.astype(F32)).astype(BF16))
    early_sum = jnp.sum(merged.astype(F32), axis=0).astype(BF16)
    late_sum = (sums[0] + late_received.astype(F32)).astype(BF16)
    return jnp.concatenate([early_sum, late_sum], axis=0)


def solution(mesh):
    in_specs = (
        P("seq", "chan"),
        P(None, None, "chan"),
        P(None, None, "chan"),
        P("chan", None),
        P("chan"),
        P("chan", None),
    )
    out_specs = P("seq", "chan")
    return jax.shard_map(body, mesh=mesh, in_specs=in_specs, out_specs=out_specs, check_vma=False)
```

```python
import jax
import jax.numpy as jnp
from jax import lax
from jax.experimental import pallas as pl
from jax.experimental.pallas import tpu as pltpu
from jax.sharding import PartitionSpec as P


YS = 8
XS = 2
LATE_IN = 128
LATE_OUT = 160
BLOCK = 32
HALO = 136
WIDE_FROM = 320 - LATE_OUT - 128 - 16
VMEM = pltpu.VMEM
F32 = jnp.float32
BF16 = jnp.bfloat16

Y_GROUPS = [[y * XS + x for y in range(YS)] for x in range(XS)]
X_PAIRS = [(y * XS + x, y * XS + 1 - x) for y in range(YS) for x in range(XS)]


def swap_x(value):
    return lax.ppermute(value, "chan", X_PAIRS)


def exchange_y(value):
    return lax.all_to_all(value, "chan", 0, 0, tiled=True, axis_index_groups=Y_GROUPS)


def shifted(value, axis):
    count = lax.axis_size(axis)
    return lax.ppermute(value, axis, [(source, source + 1) for source in range(count - 1)])


def in_vmem(value):
    return pltpu.with_memory_space_constraint(value, VMEM)


def squares_of(pieces):
    total = None
    for piece in pieces:
        wide = piece.astype(F32)
        wide = wide * wide
        part = wide[:, :128] + wide[:, 128:]
        total = part if total is None else total + part
    return total


def products(pieces, weights):
    total = None
    for piece, weight in zip(pieces, weights):
        part = jnp.dot(piece, weight, preferred_element_type=F32)
        total = part if total is None else total + part
    return total


def scale_of(squares):
    mean = jnp.sum(squares, axis=1, keepdims=True) / (YS * XS * 256)
    return lax.rsqrt(mean + 1e-06)


def start_all(copies):
    for copy in copies:
        copy.start()


def wait_all(copies):
    for copy in copies:
        copy.wait()


def own_kernel(
    x_ref, own_hbm, weight_hbm, taps, sum_hbm, squares_hbm, table_hbm,
    own, weight, sums, squares, table, arrived, sent
):
    x = x_ref[0]
    own_fetch = pltpu.make_async_copy(own_hbm, own, arrived.at[3])
    fetches = [
        pltpu.make_async_copy(weight_hbm.at[i, :, x], weight.at[i], arrived.at[i]) for i in range(3)
    ]
    start_all([own_fetch] + fetches)
    for g in range(16):
        line = jnp.broadcast_to(taps[g : g + 1, :], (BLOCK, 256))
        rolled = pltpu.roll(line, 1, 1, stride=1, stride_axis=0)
        table[BLOCK * g : BLOCK * g + BLOCK] = rolled.astype(BF16)
    own_fetch.wait()
    squares[...] = squares_of([own[y] for y in range(YS)])
    for i in range(3):
        fetches[i].wait()
        sums[i] = products([own[y] for y in range(YS)], [weight[i, y] for y in range(YS)])
    sends = [
        pltpu.make_async_copy(sums, sum_hbm, sent.at[0]),
        pltpu.make_async_copy(squares, squares_hbm, sent.at[1]),
        pltpu.make_async_copy(table, table_hbm, sent.at[2]),
    ]
    start_all(sends)
    wait_all(sends)


def other_kernel(
    x_ref, oth_hbm, weight_hbm, sum_hbm, squares_hbm, out_hbm,
    oth, weight, sums, squares, out, arrived, sent
):
    other = 1 - x_ref[0]
    oth_fetch = pltpu.make_async_copy(oth_hbm, oth, arrived.at[3])
    squares_fetch = pltpu.make_async_copy(squares_hbm, squares, arrived.at[4])
    sum_fetch = pltpu.make_async_copy(sum_hbm, sums, arrived.at[5])
    fetches = [
        pltpu.make_async_copy(weight_hbm.at[i, :, other], weight.at[i], arrived.at[i])
        for i in range(3)
    ]
    start_all([oth_fetch, squares_fetch, fetches[0], sum_fetch] + fetches[1:])
    oth_fetch.wait()
    squares_fetch.wait()
    scale = scale_of(squares[...] + squares_of([oth[y] for y in range(YS)]))
    for i in range(3):
        fetches[i].wait()
        part = products([oth[y] for y in range(YS)], [weight[i, y] for y in range(YS)])
        if i == 0:
            sum_fetch.wait()
        out[:, 256 * i : 256 * i + 256] = ((sums[i] + part) * scale).astype(BF16)
    send = pltpu.make_async_copy(out, out_hbm, sent)
    send.start()
    send.wait()


def late_kernel(x_ref, pair2, weight_hbm, proj_hbm, out_hbm, head, weight, out, arrived, sent):
    x = x_ref[0]
    late = pair2.shape[2]
    early = proj_hbm.shape[0]
    head_fetch = pltpu.make_async_copy(proj_hbm.at[early + late - HALO : early], head, arrived.at[3])
    fetches = [pltpu.make_async_copy(weight_hbm.at[i], weight.at[i], arrived.at[i]) for i in range(3)]
    start_all(fetches + [head_fetch])
    pieces = [pair2[y, side] for y in range(YS) for side in range(2)]
    scale = scale_of(squares_of(pieces))
    for i in range(3):
        fetches[i].wait()
        weights = [weight[i, y, side] for y in range(YS) for side in (x, 1 - x)]
        out[HALO - late :, 256 * i : 256 * i + 256] = (products(pieces, weights) * scale).astype(BF16)
    head_fetch.wait()
    out[0 : HALO - late] = head[...]
    send = pltpu.make_async_copy(out, out_hbm, sent)
    send.start()
    send.wait()


def mix_rows(wide, base, gated, table, short, skip, mixed, count):
    def stream(i, start, length):
        lanes = slice(256 * i, 256 * i + 256)
        total = short[0, i : i + 1, :] * wide[start : start + length, lanes]
        for back in range(1, 3):
            total += short[back, i : i + 1, :] * wide[start - back : start - back + length, lanes]
        return total

    product = stream(1, base, count + 128) * stream(2, base, count + 128)
    gated[0 : count + 128] = product.astype(BF16)
    gated[count + 128 :] = jnp.zeros((gated.shape[0] - count - 128, 256), BF16)
    group = lax.broadcasted_iota(jnp.int32, (BLOCK, 256), 1) // 16
    for b in range(count // BLOCK):
        window = gated[BLOCK * b : BLOCK * b + 256]
        every = jnp.dot(table[...], window, preferred_element_type=F32)
        total = every[0:BLOCK]
        for g in range(1, 16):
            total = jnp.where(group == g, every[BLOCK * g : BLOCK * g + BLOCK], total)
        own = gated[BLOCK * b + 128 : BLOCK * b + 128 + BLOCK].astype(F32)
        total = total + skip[...] * own
        queries = stream(0, base + 128 + BLOCK * b, BLOCK)
        mixed[BLOCK * b : BLOCK * b + BLOCK] = (queries * total).astype(BF16)


def out_rows(x, value, weight, store):
    for y in range(YS):
        mine = pl.multiple_of(y * 512 + x * 256, 256)
        other = pl.multiple_of(y * 512 + 256 - x * 256, 256)
        store(y, 0, jnp.dot(value, weight[:, pl.ds(mine, 256)], preferred_element_type=F32).astype(BF16))
        store(y, 1, jnp.dot(value, weight[:, pl.ds(other, 256)], preferred_element_type=F32).astype(BF16))


def inner_kernel(
    x_ref, proj_hbm, tail_hbm, table_hbm, short, skip, out_hbm, pair_hbm,
    proj1, tail, table, out_weight, wide, gated, mixed, pair, arrived, sent
):
    proj_fetch = pltpu.make_async_copy(proj_hbm.at[WIDE_FROM:], proj1, arrived.at[0])
    tail_fetch = pltpu.make_async_copy(tail_hbm.at[HALO - LATE_IN :], tail, arrived.at[1])
    table_fetch = pltpu.make_async_copy(table_hbm, table, arrived.at[2])
    out_fetch = pltpu.make_async_copy(out_hbm, out_weight, arrived.at[3])
    start_all([proj_fetch, tail_fetch, table_fetch, out_fetch])
    count = proj1.shape[0]
    proj_fetch.wait()
    wide[0:count] = proj1[...].astype(F32)
    tail_fetch.wait()
    wide[count:] = tail[...].astype(F32)
    table_fetch.wait()
    mix_rows(wide, 16, gated, table, short, skip, mixed, LATE_OUT)
    out_fetch.wait()
    sends = [pltpu.make_async_copy(pair.at[y], pair_hbm.at[y], sent.at[y]) for y in range(YS)]

    def place(y, side, value):
        pair[y, side] = value
        if side == 1:
            sends[y].start()

    out_rows(x_ref[0], mixed[...], out_weight, place)
    wait_all(sends)


def edge_kernel(
    x_ref, halo, proj_hbm, table_hbm, short, skip, out_hbm, send_hbm, keep_hbm,
    proj1, table, out_weight, wide, gated, mixed, send, keep, arrived, sent
):
    count = mixed.shape[0]
    proj_fetch = pltpu.make_async_copy(proj_hbm.at[0:count], proj1, arrived.at[0])
    table_fetch = pltpu.make_async_copy(table_hbm, table, arrived.at[1])
    out_fetch = pltpu.make_async_copy(out_hbm, out_weight, arrived.at[2])
    for fetch in (proj_fetch, table_fetch, out_fetch):
        fetch.start()
    wide[0:HALO] = halo[...].astype(F32)
    proj_fetch.wait()
    wide[HALO:] = proj1[...].astype(F32)
    table_fetch.wait()
    mix_rows(wide, HALO - 128, gated, table, short, skip, mixed, count)
    out_fetch.wait()

    sends = [pltpu.make_async_copy(send.at[y], send_hbm.at[y], sent.at[y]) for y in range(YS)]
    keeps = [pltpu.make_async_copy(keep.at[y], keep_hbm.at[y], sent.at[YS + y]) for y in range(YS)]

    def place(y, side, value):
        if side == 0:
            keep[y] = value
            keeps[y].start()
        else:
            send[y] = value
            sends[y].start()

    out_rows(x_ref[0], mixed[...], out_weight, place)
    wait_all(sends + keeps)


WHOLE = pl.BlockSpec(memory_space=VMEM)
ANY = pl.BlockSpec(memory_space=pltpu.HBM)
SCALAR = pl.BlockSpec(memory_space=pltpu.SMEM)
PARAMS = pltpu.CompilerParams(vmem_limit_bytes=55 << 20)


def struct(*shape):
    return jax.ShapeDtypeStruct(shape, BF16)


def body(tokens, in_weight, short_filter, long_filter, skip_gain, out_weight):
    rows = tokens.shape[0]
    early_in = rows - LATE_IN
    early_out = rows - LATE_OUT
    x = (lax.axis_index("chan") % XS).astype(jnp.int32)[None]
    weight = jnp.transpose(in_weight, (1, 0, 2)).reshape(3, YS, XS, 256, 256)
    taps = jnp.pad(jnp.flip(long_filter, 1).astype(F32), ((0, 0), (0, 128)))
    skip = skip_gain[None]

    top, tail = tokens[:early_in], tokens[early_in:]
    tail_other = swap_x(tail)
    own1 = exchange_y(jnp.broadcast_to(top[None], (YS,) + top.shape))
    oth1 = swap_x(own1)
    both = jnp.stack([tail, tail_other])
    both = jnp.broadcast_to(both[None], (YS,) + both.shape)
    pair2 = exchange_y(both)

    half_space = VMEM((3, YS, 256, 256), BF16)
    table_space = VMEM((16 * BLOCK, 256), BF16)
    out_space = VMEM(out_weight.shape, BF16)
    sum_shape = (3, early_in, 256)
    copies = pltpu.SemaphoreType.DMA
    sums, squares, table = pl.pallas_call(
        own_kernel,
        in_specs=[SCALAR, ANY, ANY, WHOLE],
        out_specs=[ANY] * 3,
        out_shape=[
            jax.ShapeDtypeStruct(sum_shape, F32),
            jax.ShapeDtypeStruct((early_in, 128), F32),
            struct(16 * BLOCK, 256),
        ],
        scratch_shapes=[
            VMEM(own1.shape, BF16),
            half_space,
            VMEM(sum_shape, F32),
            VMEM((early_in, 128), F32),
            table_space,
            copies((4,)),
            copies((3,)),
        ],
        compiler_params=PARAMS,
        name="own",
    )(x, own1, weight, taps)
    proj1 = pl.pallas_call(
        other_kernel,
        in_specs=[SCALAR, ANY, ANY, ANY, ANY],
        out_specs=ANY,
        out_shape=struct(early_in, 768),
        scratch_shapes=[
            VMEM(oth1.shape, BF16),
            half_space,
            VMEM(sum_shape, F32),
            VMEM((early_in, 128), F32),
            VMEM((early_in, 768), BF16),
            copies((6,)),
            copies,
        ],
        compiler_params=PARAMS,
        name="other",
    )(x, oth1, weight, sums, squares)
    tail_rows = pl.pallas_call(
        late_kernel,
        in_specs=[SCALAR, WHOLE, ANY, ANY],
        out_specs=ANY,
        out_shape=struct(HALO, 768),
        scratch_shapes=[
            VMEM((HALO - LATE_IN, 768), BF16),
            VMEM(weight.shape, BF16),
            VMEM((HALO, 768), BF16),
            copies((4,)),
            copies,
        ],
        compiler_params=PARAMS,
        name="late",
    )(x, in_vmem(pair2), weight, proj1)
    pair = pl.pallas_call(
        inner_kernel,
        in_specs=[SCALAR, ANY, ANY, ANY, WHOLE, WHOLE, ANY],
        out_specs=ANY,
        out_shape=struct(YS, 2, LATE_OUT, 256),
        scratch_shapes=[
            VMEM((early_in - WIDE_FROM, 768), BF16),
            VMEM((LATE_IN, 768), BF16),
            table_space,
            out_space,
            VMEM((rows - WIDE_FROM, 768), F32),
            VMEM((LATE_OUT + 256, 256), BF16),
            VMEM((LATE_OUT, 256), BF16),
            VMEM((YS, 2, LATE_OUT, 256), BF16),
            copies((4,)),
            copies((YS,)),
        ],
        compiler_params=PARAMS,
        name="inner",
    )(x, proj1, tail_rows, table, short_filter, skip, out_weight)

    halo = shifted(tail_rows, "seq")
    pair = exchange_y(pair)
    send, keep = pl.pallas_call(
        edge_kernel,
        in_specs=[SCALAR, WHOLE, ANY, ANY, WHOLE, WHOLE, ANY],
        out_specs=[ANY] * 2,
        out_shape=[struct(YS, early_out, 256), struct(YS, early_out, 256)],
        scratch_shapes=[
            VMEM((early_out, 768), BF16),
            table_space,
            out_space,
            VMEM((HALO + early_out, 768), F32),
            VMEM((early_out + 256, 256), BF16),
            VMEM((early_out, 256), BF16),
            VMEM((YS, early_out, 256), BF16),
            VMEM((YS, early_out, 256), BF16),
            copies((3,)),
            copies((2 * YS,)),
        ],
        compiler_params=PARAMS,
        name="edge",
    )(x, in_vmem(halo), proj1, table, short_filter, skip, out_weight)

    received = swap_x(send)
    sums = jnp.sum(pair.astype(F32), axis=0)
    late_send = sums[1].astype(BF16)
    late_received = swap_x(late_send)
    merged = (keep.astype(F32) + received.astype(F32)).astype(BF16)
    merged = exchange_y(merged)
    early_sum = jnp.sum(merged.astype(F32), axis=0).astype(BF16)
    late_sum = (sums[0] + late_received.astype(F32)).astype(BF16)
    return jnp.concatenate([early_sum, late_sum], axis=0)


def solution(mesh):
    in_specs = (
        P("seq", "chan"),
        P(None, None, "chan"),
        P(None, None, "chan"),
        P("chan", None),
        P("chan"),
        P("chan", None),
    )
    out_specs = P("seq", "chan")
    return jax.shard_map(body, mesh=mesh, in_specs=in_specs, out_specs=out_specs, check_vma=False)
```

```python
import jax
import jax.numpy as jnp
from jax import lax
from jax.experimental import pallas as pl
from jax.experimental.pallas import tpu as pltpu
from jax.sharding import PartitionSpec as P


YS = 8
XS = 2
LATE_IN = 112
LATE_OUT = 144
BLOCK = 16
HALO = 136
WIDE_FROM = 320 - LATE_OUT - 128 - 16
VMEM = pltpu.VMEM
F32 = jnp.float32
BF16 = jnp.bfloat16

Y_GROUPS = [[y * XS + x for y in range(YS)] for x in range(XS)]
X_PAIRS = [(y * XS + x, y * XS + 1 - x) for y in range(YS) for x in range(XS)]


def swap_x(value):
    return lax.ppermute(value, "chan", X_PAIRS)


def exchange_y(value):
    return lax.all_to_all(value, "chan", 0, 0, tiled=True, axis_index_groups=Y_GROUPS)


def shifted(value, axis):
    count = lax.axis_size(axis)
    return lax.ppermute(value, axis, [(source, source + 1) for source in range(count - 1)])


def in_vmem(value):
    return pltpu.with_memory_space_constraint(value, VMEM)


def squares_of(pieces):
    total = None
    for piece in pieces:
        wide = piece.astype(F32)
        wide = wide * wide
        part = wide[:, :128] + wide[:, 128:]
        total = part if total is None else total + part
    return total


def products(pieces, weights):
    total = None
    for piece, weight in zip(pieces, weights):
        part = jnp.dot(piece, weight, preferred_element_type=F32)
        total = part if total is None else total + part
    return total


def scale_of(squares):
    mean = jnp.sum(squares, axis=1, keepdims=True) / (YS * XS * 256)
    return lax.rsqrt(mean + 1e-06)


def start_all(copies):
    for copy in copies:
        copy.start()


def wait_all(copies):
    for copy in copies:
        copy.wait()


def spread_kernel(rows_hbm, out_hbm, sent):
    copies = [
        pltpu.make_async_copy(rows_hbm.at[0 : out_hbm.shape[1]], out_hbm.at[y], sent.at[y])
        for y in range(YS)
    ]
    start_all(copies)
    wait_all(copies)


def own_kernel(
    x_ref, own_hbm, weight_hbm, taps, sum_hbm, squares_hbm, table_hbm,
    own, weight, sums, squares, table, arrived, sent
):
    x = x_ref[0]
    own_fetch = pltpu.make_async_copy(own_hbm, own, arrived.at[3])
    fetches = [
        pltpu.make_async_copy(weight_hbm.at[i, :, x], weight.at[i], arrived.at[i]) for i in range(3)
    ]
    start_all([own_fetch] + fetches)
    for g in range(16):
        line = jnp.broadcast_to(taps[g : g + 1, :], (BLOCK, 256))
        rolled = pltpu.roll(line, 1, 1, stride=1, stride_axis=0)
        table[BLOCK * g : BLOCK * g + BLOCK] = rolled.astype(BF16)
    own_fetch.wait()
    squares[...] = squares_of([own[y] for y in range(YS)])
    for i in range(3):
        fetches[i].wait()
        sums[i] = products([own[y] for y in range(YS)], [weight[i, y] for y in range(YS)])
    sends = [
        pltpu.make_async_copy(sums, sum_hbm, sent.at[0]),
        pltpu.make_async_copy(squares, squares_hbm, sent.at[1]),
        pltpu.make_async_copy(table, table_hbm, sent.at[2]),
    ]
    start_all(sends)
    wait_all(sends)


def other_kernel(
    x_ref, oth, weight_hbm, sum_hbm, squares_hbm, out_hbm,
    weight, sums, squares, out, arrived, sent
):
    other = 1 - x_ref[0]
    squares_fetch = pltpu.make_async_copy(squares_hbm, squares, arrived.at[3])
    sum_fetch = pltpu.make_async_copy(sum_hbm, sums, arrived.at[4])
    fetches = [
        pltpu.make_async_copy(weight_hbm.at[i, :, other], weight.at[i], arrived.at[i])
        for i in range(3)
    ]
    start_all([squares_fetch, fetches[0], sum_fetch] + fetches[1:])
    squares_fetch.wait()
    scale = scale_of(squares[...] + squares_of([oth[y] for y in range(YS)]))
    for i in range(3):
        fetches[i].wait()
        part = products([oth[y] for y in range(YS)], [weight[i, y] for y in range(YS)])
        if i == 0:
            sum_fetch.wait()
        out[:, 256 * i : 256 * i + 256] = ((sums[i] + part) * scale).astype(BF16)
    send = pltpu.make_async_copy(out, out_hbm, sent)
    send.start()
    send.wait()


def late_kernel(x_ref, pair2, weight_hbm, proj_hbm, out_hbm, head, weight, out, arrived, sent):
    x = x_ref[0]
    late = pair2.shape[2]
    early = proj_hbm.shape[0]
    head_fetch = pltpu.make_async_copy(proj_hbm.at[early + late - HALO : early], head, arrived.at[3])
    fetches = [pltpu.make_async_copy(weight_hbm.at[i], weight.at[i], arrived.at[i]) for i in range(3)]
    start_all(fetches + [head_fetch])
    pieces = [pair2[y, side] for y in range(YS) for side in range(2)]
    scale = scale_of(squares_of(pieces))
    for i in range(3):
        fetches[i].wait()
        weights = [weight[i, y, side] for y in range(YS) for side in (x, 1 - x)]
        out[HALO - late :, 256 * i : 256 * i + 256] = (products(pieces, weights) * scale).astype(BF16)
    head_fetch.wait()
    out[0 : HALO - late] = head[...]
    send = pltpu.make_async_copy(out, out_hbm, sent)
    send.start()
    send.wait()


def mix_rows(wide, base, gated, table, short, skip, mixed, count):
    def stream(i, start, length):
        lanes = slice(256 * i, 256 * i + 256)
        total = short[0, i : i + 1, :] * wide[start : start + length, lanes]
        for back in range(1, 3):
            total += short[back, i : i + 1, :] * wide[start - back : start - back + length, lanes]
        return total

    product = stream(1, base, count + 128) * stream(2, base, count + 128)
    gated[0 : count + 128] = product.astype(BF16)
    gated[count + 128 :] = jnp.zeros((gated.shape[0] - count - 128, 256), BF16)
    group = lax.broadcasted_iota(jnp.int32, (BLOCK, 256), 1) // 16
    for b in range(count // BLOCK):
        window = gated[BLOCK * b : BLOCK * b + 256]
        every = jnp.dot(table[...], window, preferred_element_type=F32)
        total = every[0:BLOCK]
        for g in range(1, 16):
            total = jnp.where(group == g, every[BLOCK * g : BLOCK * g + BLOCK], total)
        own = gated[BLOCK * b + 128 : BLOCK * b + 128 + BLOCK].astype(F32)
        total = total + skip[...] * own
        queries = stream(0, base + 128 + BLOCK * b, BLOCK)
        mixed[BLOCK * b : BLOCK * b + BLOCK] = (queries * total).astype(BF16)


def out_rows(x, value, weight, store):
    for y in range(YS):
        mine = pl.multiple_of(y * 512 + x * 256, 256)
        other = pl.multiple_of(y * 512 + 256 - x * 256, 256)
        store(y, 0, jnp.dot(value, weight[:, pl.ds(mine, 256)], preferred_element_type=F32).astype(BF16))
        store(y, 1, jnp.dot(value, weight[:, pl.ds(other, 256)], preferred_element_type=F32).astype(BF16))


def inner_kernel(
    x_ref, proj_hbm, tail_hbm, table_hbm, short, skip, out_hbm, pair_hbm,
    proj1, tail, table, out_weight, wide, gated, mixed, pair, arrived, sent
):
    proj_fetch = pltpu.make_async_copy(proj_hbm.at[WIDE_FROM:], proj1, arrived.at[0])
    tail_fetch = pltpu.make_async_copy(tail_hbm.at[HALO - LATE_IN :], tail, arrived.at[1])
    table_fetch = pltpu.make_async_copy(table_hbm, table, arrived.at[2])
    out_fetch = pltpu.make_async_copy(out_hbm, out_weight, arrived.at[3])
    start_all([proj_fetch, tail_fetch, table_fetch, out_fetch])
    count = proj1.shape[0]
    proj_fetch.wait()
    wide[0:count] = proj1[...].astype(F32)
    tail_fetch.wait()
    wide[count:] = tail[...].astype(F32)
    table_fetch.wait()
    mix_rows(wide, 16, gated, table, short, skip, mixed, LATE_OUT)
    out_fetch.wait()
    sends = [pltpu.make_async_copy(pair.at[y], pair_hbm.at[y], sent.at[y]) for y in range(YS)]

    def place(y, side, value):
        pair[y, side] = value
        if side == 1:
            sends[y].start()

    out_rows(x_ref[0], mixed[...], out_weight, place)
    wait_all(sends)


def edge_kernel(
    x_ref, halo, proj_hbm, table_hbm, short, skip, out_hbm, send_hbm, keep_hbm,
    proj1, table, out_weight, wide, gated, mixed, send, keep, arrived, sent
):
    count = mixed.shape[0]
    proj_fetch = pltpu.make_async_copy(proj_hbm.at[0:count], proj1, arrived.at[0])
    table_fetch = pltpu.make_async_copy(table_hbm, table, arrived.at[1])
    out_fetch = pltpu.make_async_copy(out_hbm, out_weight, arrived.at[2])
    for fetch in (proj_fetch, table_fetch, out_fetch):
        fetch.start()
    wide[0:HALO] = halo[...].astype(F32)
    proj_fetch.wait()
    wide[HALO:] = proj1[...].astype(F32)
    table_fetch.wait()
    mix_rows(wide, HALO - 128, gated, table, short, skip, mixed, count)
    out_fetch.wait()

    sends = [pltpu.make_async_copy(send.at[y], send_hbm.at[y], sent.at[y]) for y in range(YS)]
    keeps = [pltpu.make_async_copy(keep.at[y], keep_hbm.at[y], sent.at[YS + y]) for y in range(YS)]

    def place(y, side, value):
        if side == 0:
            keep[y] = value
            keeps[y].start()
        else:
            send[y] = value
            sends[y].start()

    out_rows(x_ref[0], mixed[...], out_weight, place)
    wait_all(sends + keeps)


WHOLE = pl.BlockSpec(memory_space=VMEM)
ANY = pl.BlockSpec(memory_space=pltpu.HBM)
SCALAR = pl.BlockSpec(memory_space=pltpu.SMEM)
PARAMS = pltpu.CompilerParams(vmem_limit_bytes=55 << 20)


def struct(*shape):
    return jax.ShapeDtypeStruct(shape, BF16)


def body(tokens, in_weight, short_filter, long_filter, skip_gain, out_weight):
    rows = tokens.shape[0]
    early_in = rows - LATE_IN
    early_out = rows - LATE_OUT
    x = (lax.axis_index("chan") % XS).astype(jnp.int32)[None]
    weight = jnp.transpose(in_weight, (1, 0, 2)).reshape(3, YS, XS, 256, 256)
    taps = jnp.pad(jnp.flip(long_filter, 1).astype(F32), ((0, 0), (0, 128)))
    skip = skip_gain[None]

    copies = pltpu.SemaphoreType.DMA
    tail = tokens[early_in:]
    top = pl.pallas_call(
        spread_kernel,
        in_specs=[ANY],
        out_specs=ANY,
        out_shape=struct(YS, early_in, 256),
        scratch_shapes=[copies((YS,))],
        compiler_params=PARAMS,
        name="top",
    )(tokens)
    tail_other = swap_x(tail)
    own1 = exchange_y(top)
    oth1 = swap_x(own1)
    both = jnp.stack([tail, tail_other])
    both = jnp.broadcast_to(both[None], (YS,) + both.shape)
    pair2 = exchange_y(both)

    half_space = VMEM((3, YS, 256, 256), BF16)
    table_space = VMEM((16 * BLOCK, 256), BF16)
    out_space = VMEM(out_weight.shape, BF16)
    sum_shape = (3, early_in, 256)
    sums, squares, table = pl.pallas_call(
        own_kernel,
        in_specs=[SCALAR, ANY, ANY, WHOLE],
        out_specs=[ANY] * 3,
        out_shape=[
            jax.ShapeDtypeStruct(sum_shape, F32),
            jax.ShapeDtypeStruct((early_in, 128), F32),
            struct(16 * BLOCK, 256),
        ],
        scratch_shapes=[
            VMEM(own1.shape, BF16),
            half_space,
            VMEM(sum_shape, F32),
            VMEM((early_in, 128), F32),
            table_space,
            copies((4,)),
            copies((3,)),
        ],
        compiler_params=PARAMS,
        name="own",
    )(x, own1, weight, taps)
    proj1 = pl.pallas_call(
        other_kernel,
        in_specs=[SCALAR, WHOLE, ANY, ANY, ANY],
        out_specs=ANY,
        out_shape=struct(early_in, 768),
        scratch_shapes=[
            half_space,
            VMEM(sum_shape, F32),
            VMEM((early_in, 128), F32),
            VMEM((early_in, 768), BF16),
            copies((5,)),
            copies,
        ],
        compiler_params=PARAMS,
        name="other",
    )(x, in_vmem(oth1), weight, sums, squares)
    tail_rows = pl.pallas_call(
        late_kernel,
        in_specs=[SCALAR, WHOLE, ANY, ANY],
        out_specs=ANY,
        out_shape=struct(HALO, 768),
        scratch_shapes=[
            VMEM((HALO - LATE_IN, 768), BF16),
            VMEM(weight.shape, BF16),
            VMEM((HALO, 768), BF16),
            copies((4,)),
            copies,
        ],
        compiler_params=PARAMS,
        name="late",
    )(x, in_vmem(pair2), weight, proj1)
    pair = pl.pallas_call(
        inner_kernel,
        in_specs=[SCALAR, ANY, ANY, ANY, WHOLE, WHOLE, ANY],
        out_specs=ANY,
        out_shape=struct(YS, 2, LATE_OUT, 256),
        scratch_shapes=[
            VMEM((early_in - WIDE_FROM, 768), BF16),
            VMEM((LATE_IN, 768), BF16),
            table_space,
            out_space,
            VMEM((rows - WIDE_FROM, 768), F32),
            VMEM((LATE_OUT + 256, 256), BF16),
            VMEM((LATE_OUT, 256), BF16),
            VMEM((YS, 2, LATE_OUT, 256), BF16),
            copies((4,)),
            copies((YS,)),
        ],
        compiler_params=PARAMS,
        name="inner",
    )(x, proj1, tail_rows, table, short_filter, skip, out_weight)

    halo = shifted(tail_rows, "seq")
    pair = exchange_y(pair)
    send, keep = pl.pallas_call(
        edge_kernel,
        in_specs=[SCALAR, WHOLE, ANY, ANY, WHOLE, WHOLE, ANY],
        out_specs=[ANY] * 2,
        out_shape=[struct(YS, early_out, 256), struct(YS, early_out, 256)],
        scratch_shapes=[
            VMEM((early_out, 768), BF16),
            table_space,
            out_space,
            VMEM((HALO + early_out, 768), F32),
            VMEM((early_out + 256, 256), BF16),
            VMEM((early_out, 256), BF16),
            VMEM((YS, early_out, 256), BF16),
            VMEM((YS, early_out, 256), BF16),
            copies((3,)),
            copies((2 * YS,)),
        ],
        compiler_params=PARAMS,
        name="edge",
    )(x, in_vmem(halo), proj1, table, short_filter, skip, out_weight)

    received = swap_x(send)
    sums = jnp.sum(pair.astype(F32), axis=0)
    late_send = sums[1].astype(BF16)
    late_received = swap_x(late_send)
    merged = (keep.astype(F32) + received.astype(F32)).astype(BF16)
    merged = exchange_y(merged)
    early_sum = jnp.sum(merged.astype(F32), axis=0).astype(BF16)
    late_sum = (sums[0] + late_received.astype(F32)).astype(BF16)
    return jnp.concatenate([early_sum, late_sum], axis=0)


def solution(mesh):
    in_specs = (
        P("seq", "chan"),
        P(None, None, "chan"),
        P(None, None, "chan"),
        P("chan", None),
        P("chan"),
        P("chan", None),
    )
    out_specs = P("seq", "chan")
    return jax.shard_map(body, mesh=mesh, in_specs=in_specs, out_specs=out_specs, check_vma=False)
```

```python
import jax
import jax.numpy as jnp
from jax import lax
from jax.experimental import pallas as pl
from jax.experimental.pallas import tpu as pltpu
from jax.sharding import PartitionSpec as P


YS = 8
XS = 2
LATE_IN = 128
LATE_OUT = 160
BLOCK = 16
HALO = 136
WIDE_FROM = 320 - LATE_OUT - 128 - 16
VMEM = pltpu.VMEM
F32 = jnp.float32
BF16 = jnp.bfloat16

Y_GROUPS = [[y * XS + x for y in range(YS)] for x in range(XS)]
X_PAIRS = [(y * XS + x, y * XS + 1 - x) for y in range(YS) for x in range(XS)]


def swap_x(value):
    return lax.ppermute(value, "chan", X_PAIRS)


def exchange_y(value):
    return lax.all_to_all(value, "chan", 0, 0, tiled=True, axis_index_groups=Y_GROUPS)


def shifted(value, axis):
    count = lax.axis_size(axis)
    return lax.ppermute(value, axis, [(source, source + 1) for source in range(count - 1)])


def in_vmem(value):
    return pltpu.with_memory_space_constraint(value, VMEM)


def squares_of(pieces):
    total = None
    for piece in pieces:
        wide = piece.astype(F32)
        wide = wide * wide
        part = wide[:, :128] + wide[:, 128:]
        total = part if total is None else total + part
    return total


def products(pieces, weights):
    total = None
    for piece, weight in zip(pieces, weights):
        part = jnp.dot(piece, weight, preferred_element_type=F32)
        total = part if total is None else total + part
    return total


def scale_of(squares):
    mean = jnp.sum(squares, axis=1, keepdims=True) / (YS * XS * 256)
    return lax.rsqrt(mean + 1e-06)


def start_all(copies):
    for copy in copies:
        copy.start()


def wait_all(copies):
    for copy in copies:
        copy.wait()


def spread_kernel(rows_hbm, out_hbm, rows, sent):
    fetch = pltpu.make_async_copy(rows_hbm.at[0 : rows.shape[0]], rows, sent.at[YS])
    fetch.start()
    fetch.wait()
    copies = [pltpu.make_async_copy(rows, out_hbm.at[y], sent.at[y]) for y in range(YS)]
    start_all(copies)
    wait_all(copies)


def slab_kernel(x_ref, weight_hbm, out_hbm, slab, arrived, sent):
    other = 1 - x_ref[0]
    fetches = []
    sends = []
    for y in range(YS):
        first = pl.multiple_of(y * 512 + other * 256, 256)
        fetches.append(
            pltpu.make_async_copy(weight_hbm.at[:, pl.ds(first, 256)], slab.at[y], arrived.at[y])
        )
        sends.append(pltpu.make_async_copy(slab.at[y], out_hbm.at[y], sent.at[y]))
    start_all(fetches)
    for y in range(YS):
        fetches[y].wait()
        sends[y].start()
    wait_all(sends)


def own_kernel(
    x_ref, own_hbm, weight_hbm, taps, sum_hbm, squares_hbm, table_hbm,
    own, weight, sums, squares, table, arrived, sent
):
    x = x_ref[0]
    own_fetch = pltpu.make_async_copy(own_hbm, own, arrived.at[3])
    fetches = [
        pltpu.make_async_copy(weight_hbm.at[i, :, x], weight.at[i], arrived.at[i]) for i in range(3)
    ]
    start_all([own_fetch] + fetches)
    for g in range(16):
        line = jnp.broadcast_to(taps[g : g + 1, :], (BLOCK, 256))
        rolled = pltpu.roll(line, 1, 1, stride=1, stride_axis=0)
        table[BLOCK * g : BLOCK * g + BLOCK] = rolled.astype(BF16)
    own_fetch.wait()
    squares[...] = squares_of([own[y] for y in range(YS)])
    for i in range(3):
        fetches[i].wait()
        sums[i] = products([own[y] for y in range(YS)], [weight[i, y] for y in range(YS)])
    sends = [
        pltpu.make_async_copy(sums, sum_hbm, sent.at[0]),
        pltpu.make_async_copy(squares, squares_hbm, sent.at[1]),
        pltpu.make_async_copy(table, table_hbm, sent.at[2]),
    ]
    start_all(sends)
    wait_all(sends)


def other_kernel(
    x_ref, oth, weight_hbm, sum_hbm, squares_hbm, out_hbm,
    weight, sums, squares, out, arrived, sent
):
    other = 1 - x_ref[0]
    squares_fetch = pltpu.make_async_copy(squares_hbm, squares, arrived.at[3])
    sum_fetch = pltpu.make_async_copy(sum_hbm, sums, arrived.at[4])
    fetches = [
        pltpu.make_async_copy(weight_hbm.at[i, :, other], weight.at[i], arrived.at[i])
        for i in range(3)
    ]
    start_all([squares_fetch, fetches[0], sum_fetch] + fetches[1:])
    squares_fetch.wait()
    scale = scale_of(squares[...] + squares_of([oth[y] for y in range(YS)]))
    for i in range(3):
        fetches[i].wait()
        part = products([oth[y] for y in range(YS)], [weight[i, y] for y in range(YS)])
        if i == 0:
            sum_fetch.wait()
        out[:, 256 * i : 256 * i + 256] = ((sums[i] + part) * scale).astype(BF16)
    send = pltpu.make_async_copy(out, out_hbm, sent)
    send.start()
    send.wait()


def late_kernel(x_ref, pair2, weight_hbm, proj_hbm, out_hbm, head, weight, out, arrived, sent):
    x = x_ref[0]
    late = pair2.shape[2]
    early = proj_hbm.shape[0]
    head_fetch = pltpu.make_async_copy(proj_hbm.at[early + late - HALO : early], head, arrived.at[3])
    fetches = [pltpu.make_async_copy(weight_hbm.at[i], weight.at[i], arrived.at[i]) for i in range(3)]
    start_all(fetches + [head_fetch])
    pieces = [pair2[y, side] for y in range(YS) for side in range(2)]
    scale = scale_of(squares_of(pieces))
    for i in range(3):
        fetches[i].wait()
        weights = [weight[i, y, side] for y in range(YS) for side in (x, 1 - x)]
        out[HALO - late :, 256 * i : 256 * i + 256] = (products(pieces, weights) * scale).astype(BF16)
    head_fetch.wait()
    out[0 : HALO - late] = head[...]
    send = pltpu.make_async_copy(out, out_hbm, sent)
    send.start()
    send.wait()


def mix_rows(wide, base, gated, table, short, skip, mixed, count):
    def stream(i, start, length):
        lanes = slice(256 * i, 256 * i + 256)
        total = short[0, i : i + 1, :] * wide[start : start + length, lanes]
        for back in range(1, 3):
            total += short[back, i : i + 1, :] * wide[start - back : start - back + length, lanes]
        return total

    product = stream(1, base, count + 128) * stream(2, base, count + 128)
    gated[0 : count + 128] = product.astype(BF16)
    gated[count + 128 :] = jnp.zeros((gated.shape[0] - count - 128, 256), BF16)
    group = lax.broadcasted_iota(jnp.int32, (BLOCK, 256), 1) // 16
    for b in range(count // BLOCK):
        window = gated[BLOCK * b : BLOCK * b + 256]
        every = jnp.dot(table[...], window, preferred_element_type=F32)
        total = every[0:BLOCK]
        for g in range(1, 16):
            total = jnp.where(group == g, every[BLOCK * g : BLOCK * g + BLOCK], total)
        own = gated[BLOCK * b + 128 : BLOCK * b + 128 + BLOCK].astype(F32)
        total = total + skip[...] * own
        queries = stream(0, base + 128 + BLOCK * b, BLOCK)
        mixed[BLOCK * b : BLOCK * b + BLOCK] = (queries * total).astype(BF16)


def inner_kernel(
    proj_hbm, tail_hbm, table_hbm, short, skip, mixed_hbm,
    proj1, tail, table, wide, gated, mixed, arrived
):
    proj_fetch = pltpu.make_async_copy(proj_hbm.at[WIDE_FROM:], proj1, arrived.at[0])
    tail_fetch = pltpu.make_async_copy(tail_hbm.at[HALO - LATE_IN :], tail, arrived.at[1])
    table_fetch = pltpu.make_async_copy(table_hbm, table, arrived.at[2])
    start_all([proj_fetch, tail_fetch, table_fetch])
    count = proj1.shape[0]
    proj_fetch.wait()
    wide[0:count] = proj1[...].astype(F32)
    tail_fetch.wait()
    wide[count:] = tail[...].astype(F32)
    table_fetch.wait()
    mix_rows(wide, 16, gated, table, short, skip, mixed, mixed.shape[0])
    send = pltpu.make_async_copy(mixed, mixed_hbm, arrived.at[3])
    send.start()
    send.wait()


def edge_kernel(
    halo, proj_hbm, table_hbm, short, skip, mixed_hbm, proj1, table, wide, gated, mixed, arrived
):
    count = mixed.shape[0]
    proj_fetch = pltpu.make_async_copy(proj_hbm.at[0:count], proj1, arrived.at[0])
    table_fetch = pltpu.make_async_copy(table_hbm, table, arrived.at[1])
    start_all([proj_fetch, table_fetch])
    wide[0:HALO] = halo[...].astype(F32)
    proj_fetch.wait()
    wide[HALO:] = proj1[...].astype(F32)
    table_fetch.wait()
    mix_rows(wide, HALO - 128, gated, table, short, skip, mixed, count)
    send = pltpu.make_async_copy(mixed, mixed_hbm, arrived.at[2])
    send.start()
    send.wait()


def sums_kernel(x_ref, own_hbm, oth, weight_hbm, slab_hbm, out_hbm, own, weight, slab, out, arrived, sent):
    x = x_ref[0]
    own_fetch = pltpu.make_async_copy(own_hbm, own, arrived.at[2 * YS])
    own_fetch.start()
    fetches = []
    sends = []
    for y in range(YS):
        first = pl.multiple_of(y * 512 + x * 256, 256)
        fetches.append(
            pltpu.make_async_copy(weight_hbm.at[:, pl.ds(first, 256)], weight.at[y], arrived.at[y])
        )
        fetches.append(pltpu.make_async_copy(slab_hbm.at[y], slab.at[y], arrived.at[YS + y]))
        sends.append(pltpu.make_async_copy(out.at[y], out_hbm.at[y], sent.at[y]))
    start_all(fetches)
    own_fetch.wait()
    for y in range(YS):
        wait_all(fetches[2 * y : 2 * y + 2])
        total = jnp.dot(own[...], weight[y], preferred_element_type=F32)
        total = total + jnp.dot(oth[...], slab[y], preferred_element_type=F32)
        out[y] = total.astype(BF16)
        sends[y].start()
    wait_all(sends)


WHOLE = pl.BlockSpec(memory_space=VMEM)
ANY = pl.BlockSpec(memory_space=pltpu.HBM)
SCALAR = pl.BlockSpec(memory_space=pltpu.SMEM)
PARAMS = pltpu.CompilerParams(vmem_limit_bytes=55 << 20)


def struct(*shape):
    return jax.ShapeDtypeStruct(shape, BF16)


def body(tokens, in_weight, short_filter, long_filter, skip_gain, out_weight):
    rows = tokens.shape[0]
    early_in = rows - LATE_IN
    early_out = rows - LATE_OUT
    x = (lax.axis_index("chan") % XS).astype(jnp.int32)[None]
    weight = jnp.transpose(in_weight, (1, 0, 2)).reshape(3, YS, XS, 256, 256)
    taps = jnp.pad(jnp.flip(long_filter, 1).astype(F32), ((0, 0), (0, 128)))
    skip = skip_gain[None]

    copies = pltpu.SemaphoreType.DMA
    tail = tokens[early_in:]
    top = pl.pallas_call(
        spread_kernel,
        in_specs=[ANY],
        out_specs=ANY,
        out_shape=struct(YS, early_in, 256),
        scratch_shapes=[VMEM((early_in, 256), BF16), copies((YS + 1,))],
        compiler_params=PARAMS,
        name="top",
    )(tokens)
    tail_other = swap_x(tail)
    slab_shape = (YS, 256, 256)
    slab = pl.pallas_call(
        slab_kernel,
        in_specs=[SCALAR, ANY],
        out_specs=ANY,
        out_shape=struct(*slab_shape),
        scratch_shapes=[VMEM(slab_shape, BF16), copies((YS,)), copies((YS,))],
        compiler_params=PARAMS,
        name="slab",
    )(x, out_weight)
    slab = swap_x(slab)
    own1 = exchange_y(top)
    oth1 = swap_x(own1)
    both = jnp.stack([tail, tail_other])
    both = jnp.broadcast_to(both[None], (YS,) + both.shape)
    pair2 = exchange_y(both)

    half_space = VMEM((3, YS, 256, 256), BF16)
    table_space = VMEM((16 * BLOCK, 256), BF16)
    sum_shape = (3, early_in, 256)
    sums, squares, table = pl.pallas_call(
        own_kernel,
        in_specs=[SCALAR, ANY, ANY, WHOLE],
        out_specs=[ANY] * 3,
        out_shape=[
            jax.ShapeDtypeStruct(sum_shape, F32),
            jax.ShapeDtypeStruct((early_in, 128), F32),
            struct(16 * BLOCK, 256),
        ],
        scratch_shapes=[
            VMEM(own1.shape, BF16),
            half_space,
            VMEM(sum_shape, F32),
            VMEM((early_in, 128), F32),
            table_space,
            copies((4,)),
            copies((3,)),
        ],
        compiler_params=PARAMS,
        name="own",
    )(x, own1, weight, taps)
    proj1 = pl.pallas_call(
        other_kernel,
        in_specs=[SCALAR, WHOLE, ANY, ANY, ANY],
        out_specs=ANY,
        out_shape=struct(early_in, 768),
        scratch_shapes=[
            half_space,
            VMEM(sum_shape, F32),
            VMEM((early_in, 128), F32),
            VMEM((early_in, 768), BF16),
            copies((5,)),
            copies,
        ],
        compiler_params=PARAMS,
        name="other",
    )(x, in_vmem(oth1), weight, sums, squares)
    tail_rows = pl.pallas_call(
        late_kernel,
        in_specs=[SCALAR, WHOLE, ANY, ANY],
        out_specs=ANY,
        out_shape=struct(HALO, 768),
        scratch_shapes=[
            VMEM((HALO - LATE_IN, 768), BF16),
            VMEM(weight.shape, BF16),
            VMEM((HALO, 768), BF16),
            copies((4,)),
            copies,
        ],
        compiler_params=PARAMS,
        name="late",
    )(x, in_vmem(pair2), weight, proj1)
    late_mixed = pl.pallas_call(
        inner_kernel,
        in_specs=[ANY, ANY, ANY, WHOLE, WHOLE],
        out_specs=ANY,
        out_shape=struct(LATE_OUT, 256),
        scratch_shapes=[
            VMEM((early_in - WIDE_FROM, 768), BF16),
            VMEM((LATE_IN, 768), BF16),
            table_space,
            VMEM((rows - WIDE_FROM, 768), F32),
            VMEM((LATE_OUT + 256, 256), BF16),
            VMEM((LATE_OUT, 256), BF16),
            copies((4,)),
        ],
        compiler_params=PARAMS,
        name="inner",
    )(proj1, tail_rows, table, short_filter, skip)

    def column_sums(own, oth):
        count = own.shape[0]
        return pl.pallas_call(
            sums_kernel,
            in_specs=[SCALAR, ANY, WHOLE, ANY, ANY],
            out_specs=ANY,
            out_shape=struct(YS, count, 256),
            scratch_shapes=[
                VMEM((count, 256), BF16),
                VMEM(slab_shape, BF16),
                VMEM(slab_shape, BF16),
                VMEM((YS, count, 256), BF16),
                copies((2 * YS + 1,)),
                copies((YS,)),
            ],
            compiler_params=PARAMS,
        )(x, own, in_vmem(oth), out_weight, slab)

    halo = shifted(tail_rows, "seq")
    late_other = swap_x(late_mixed)
    late_sums = column_sums(late_mixed, late_other)
    late_sums = exchange_y(late_sums)
    edge_mixed = pl.pallas_call(
        edge_kernel,
        in_specs=[WHOLE, ANY, ANY, WHOLE, WHOLE],
        out_specs=ANY,
        out_shape=struct(early_out, 256),
        scratch_shapes=[
            VMEM((early_out, 768), BF16),
            table_space,
            VMEM((HALO + early_out, 768), F32),
            VMEM((early_out + 256, 256), BF16),
            VMEM((early_out, 256), BF16),
            copies((3,)),
        ],
        compiler_params=PARAMS,
        name="edge",
    )(in_vmem(halo), proj1, table, short_filter, skip)
    edge_other = swap_x(edge_mixed)
    edge_sums = column_sums(edge_mixed, edge_other)
    edge_sums = exchange_y(edge_sums)
    late_total = jnp.sum(late_sums.astype(F32), axis=0).astype(BF16)
    edge_total = jnp.sum(edge_sums.astype(F32), axis=0).astype(BF16)
    return jnp.concatenate([edge_total, late_total], axis=0)


def solution(mesh):
    in_specs = (
        P("seq", "chan"),
        P(None, None, "chan"),
        P(None, None, "chan"),
        P("chan", None),
        P("chan"),
        P("chan", None),
    )
    out_specs = P("seq", "chan")
    return jax.shard_map(body, mesh=mesh, in_specs=in_specs, out_specs=out_specs, check_vma=False)
```
